32 devices in a mesh: space: 4 (over z), expert: 4 (over y, x), mp: 2 (over core).
Axes of the slice: x: 2, y: 2, z: 4, core: 2. Of those that a mesh axis runs over, the one named last changes fastest.
Arguments:
- tokens: bfloat16 [4, 32, 8, 8, 1024], P('expert', 'space'), may hold values from -6 to 6
- shifts: int32 [4], P('expert'), may hold values from 1 to 7
- regimes: int32 [4, 32, 8, 8, 1], P('expert', 'space'), may hold values from 0 to 3; in each aligned block of 512 rows (0 to 511, 512 to 1023, ..., all dimensions but the last counted through in order) at most 256 rows name the same one
- norm1_gain: float32 [1024], replicated, may hold values from 0.1 to 1.9
- qkv_weight: bfloat16 [1024, 3, 512], P(None, None, 'mp'), may hold values from -1 to 1
- out_weight: bfloat16 [512, 1024], P('mp'), may hold values from -0.5 to 0.5
- norm2_gain: float32 [1024], replicated, may hold values from 0.1 to 1.9
- w_in: bfloat16 [4, 1024, 2048], P('expert', 'space', 'mp'), may hold values from -0.1875 to 0.1875
- w_out: bfloat16 [4, 1024, 2048], P('expert', 'space', 'mp'), may hold values from -0.1875 to 0.1875
Outputs:
- result: bfloat16 [4, 32, 8, 8, 1024], P('expert', 'space')
The draws below stay inside these ranges and needn't reach their ends.
Inputs may be any that keep to these rules, and one draw needn't show every extreme that they name: `regimes`: in the 512 tokens of each slab (8 consecutive planes of one sample), at most 256 name the same expert, and on some slab some expert is named by exactly 256.
All inputs are finite; a program needn't handle non-finite values.
Results may differ from the reference program's by a relative error of at most 0.014.
Values may be sent and summed in bfloat16 or wider, within the bound.
A program may use at most 64 MiB of HBM per device.

```python
import math
import jax
import jax.numpy as jnp
import numpy as np
from jax import lax

D = 1024
HEADS = 16
HEAD_DIM = 32
FF = 2048
WIN = 8
NX = 32
SAMPLES = 4
TOK_DEV = 512
EXPERTS = 4
CAP = 256
N_SPACE = 4
N_MP = 2


def draw_qkv_weight(key, part):
    width = HEADS * HEAD_DIM
    base = jax.random.truncated_normal(key, -4.0, 4.0, (D, 3, width), jnp.float32) * jnp.sqrt(3.0 / D)
    return base.astype(jnp.bfloat16)


def set_ends(array, key, smallest, high):
    spot = [jax.random.randint(jax.random.fold_in(key, axis), (), 0, length) for axis, length in enumerate(array.shape)]
    main_axis = array.shape.index(max(array.shape))
    next_to = spot[:main_axis] + [(spot[main_axis] + 1) % array.shape[main_axis]] + spot[main_axis + 1:]
    return array.at[tuple(spot)].set(smallest).at[tuple(next_to)].set(high)


def block_scale(key, dims, cuts, low, top_value):
    loudness, own = 1.0, jax.random.fold_in(key, 6)
    for axis_at, parts in cuts:
        draws = jnp.exp(jax.random.uniform(jax.random.fold_in(own, axis_at), (parts,), jnp.float32, low / len(cuts), top_value / len(cuts)))
        loudness = loudness * jnp.repeat(draws, dims[axis_at] // parts).reshape([-1 if axis == axis_at else 1 for axis in range(len(dims))])
    return loudness


def shared_out(key, own, number, rows, count, top, reach, skew):
    ranking = jax.random.permutation(key, count)
    packed, ordinary = load_shares(count, rows * top, reach, skew, True), load_shares(count, rows * top, reach, skew, False)
    places = jnp.arange(count)

    def named(lengths, offset_by):
        used = int((lengths > 0).sum())
        fixed = max(1, used // 4)
        moved = fixed + (places - fixed + offset_by * (used - fixed)) % max(1, count - fixed)
        return jnp.zeros((count,), jnp.int32).at[ranking[jnp.where(places < fixed, places, moved)]].set(jnp.asarray(lengths, jnp.int32))

    lengths = jnp.where(number % 4 == 0, named(packed, number // 4), named(ordinary, number - number // 4 - 1))
    mixed = jax.random.permutation(jax.random.fold_in(own, 3), count)
    donor, taker = mixed[0:count // 2 * 2:2], mixed[1:count // 2 * 2:2]
    margin = jnp.minimum(lengths[donor] - 1, reach - lengths[taker]) // 2
    margin = jnp.where((donor == ranking[0]) | (taker == ranking[0]) | (lengths[taker] == 0), 0, jnp.maximum(margin, 0))
    moved = jax.random.randint(jax.random.fold_in(own, 4), (count // 2,), 0, 1 << 20) % (margin + 1)
    lengths = lengths.at[donor].add(-moved).at[taker].add(moved)
    members = jnp.searchsorted(jnp.cumsum(lengths), jnp.arange(rows * top), side="right").astype(jnp.int32)
    table = members.reshape(top, rows).T
    table = table[jax.random.permutation(jax.random.fold_in(own, 1), rows)]
    offset_by = jax.random.randint(jax.random.fold_in(own, 2), (rows, 1), 0, top)
    return jnp.take_along_axis(table, (jnp.arange(top)[None, :] + offset_by) % top, axis=1)


def load_shares(count, total, limit, lean, full):
    portions = [(1 << 20) // math.isqrt(standing ** lean) + 1 for standing in range(1, count + 1)]
    largest = limit if full else min(limit, max(-(-total // count), total * portions[0] // sum(portions)))
    least = 1 if total - largest >= count - 1 else 0
    counts, rest = [largest] + [least] * (count - 1), total - largest - least * (count - 1)
    while rest > 0:
        free = [i for i in range(1, count) if counts[i] < largest] or [i for i in range(1, count) if counts[i] < limit]
        mass, budget = sum([portions[i] for i in free]), rest
        for i in free:
            addition = min(limit - counts[i], max(1, budget * portions[i] // mass), rest)
            counts[i] = counts[i] + addition
            rest = rest - addition
    return np.array(counts)


def noise(key, extent, deviation, most, pieces=(), kind=jnp.bfloat16):
    values = deviation * jax.random.normal(key, extent, jnp.float32)
    if pieces:
        values = values * block_scale(key, extent, pieces, -0.22, 0.18)
    return jnp.clip(values, -most, most).astype(kind)


def setup_inputs(seed: int = 0) -> dict:
    seeds = jax.random.split(jax.random.key(seed), 10)
    tokens = noise(seeds[0], (SAMPLES, NX, WIN, WIN, D), 1.0, 6.0, ((0, 4), (1, 4)))
    shifts = set_ends(jax.random.randint(seeds[1], (SAMPLES,), 1, WIN), jax.random.fold_in(seeds[1], 1), 1, WIN - 1).astype(jnp.int32)
    regimes_keys = jax.random.split(jax.random.fold_in(seeds[2], 1), SAMPLES * NX * WIN * WIN // TOK_DEV)
    regimes_turns = jax.random.permutation(jax.random.fold_in(seeds[2], 3), SAMPLES * NX * WIN * WIN // TOK_DEV)
    regimes = jax.vmap(lambda own, number: shared_out(jax.random.fold_in(seeds[2], 2), own, number, TOK_DEV, EXPERTS, 1, CAP, 2))(regimes_keys, regimes_turns).reshape((SAMPLES, NX, WIN, WIN, 1))
    norm1_gain = jnp.clip(1.0 + 0.18 * jax.random.normal(seeds[3], (D,), jnp.float32), 0.1, 1.9)
    qkv_weight = draw_qkv_weight(jax.random.fold_in(seeds[9], 71), 0)
    out_weight = noise(seeds[5], (HEADS * HEAD_DIM, D), (HEADS * HEAD_DIM // 4) ** -0.5, 0.5, ((0, 2),))
    norm2_gain = jnp.clip(1.0 + 0.18 * jax.random.normal(seeds[6], (D,), jnp.float32), 0.1, 1.9)
    w_in = noise(seeds[7], (EXPERTS, D, FF), D ** -0.5, 0.1875, ((0, 4), (1, 4), (2, 2)))
    w_out = noise(seeds[8], (EXPERTS, D, FF), (FF // 2) ** -0.5, 0.1875, ((0, 4), (1, 4), (2, 2)))
    return {"tokens": tokens, "shifts": shifts, "regimes": regimes, "norm1_gain": norm1_gain, "qkv_weight": qkv_weight, "out_weight": out_weight, "norm2_gain": norm2_gain, "w_in": w_in, "w_out": w_out}


EPS = 1e-05

def layer_norm(values, gain):
    values = values.astype(jnp.float32)
    center = values - lax.optimization_barrier(jnp.mean(values, axis=-1, keepdims=True))
    spread = lax.optimization_barrier(jnp.mean(center * center, axis=-1, keepdims=True))
    return center * lax.rsqrt(spread + EPS) * gain.astype(jnp.float32)

def one_window(part):
    query = part[:, 0].astype(jnp.float32)
    keys = part[:, 1].astype(jnp.float32)
    values = part[:, 2].astype(jnp.float32)
    scores = jnp.einsum('phc,qhc->hpq', query, keys) * HEAD_DIM ** (-0.5)
    peak = lax.optimization_barrier(jnp.max(scores, axis=-1, keepdims=True))
    weights = jnp.exp(scores - peak)
    total = lax.optimization_barrier(jnp.sum(weights, axis=-1, keepdims=True))
    probabilities = (weights / total).astype(jnp.bfloat16)
    context = jnp.einsum('hpq,qhc->phc', probabilities.astype(jnp.float32), values)
    return context.astype(jnp.bfloat16).reshape(part.shape[0], HEADS * HEAD_DIM)

def reference(tokens, shifts, regimes, norm1_gain, qkv_weight, out_weight, norm2_gain, w_in, w_out):
    cube = WIN * WIN * WIN
    grid_rows = NX * WIN * WIN
    group_width = HEADS * HEAD_DIM // N_MP
    half_hidden = FF // N_MP

    def attend(args):
        sample, offset = args
        rolled = jnp.roll(sample, -offset, axis=0)
        normed = layer_norm(rolled.reshape(grid_rows, D), norm1_gain).astype(jnp.bfloat16)
        projected = jnp.einsum('rd,dkc->rkc', normed.astype(jnp.float32), qkv_weight.astype(jnp.float32)).astype(jnp.bfloat16)
        windows = projected.reshape(NX // WIN, cube, 3, HEADS, HEAD_DIM)
        context = lax.map(one_window, windows).reshape(grid_rows, N_MP, group_width)
        head_parts = jnp.einsum('rgc,gcd->rgd', context.astype(jnp.float32), out_weight.reshape(N_MP, group_width, D).astype(jnp.float32)).astype(jnp.bfloat16)
        attended = lax.optimization_barrier(jnp.sum(head_parts.astype(jnp.float32), axis=1)).reshape(NX, WIN, WIN, D)
        attended = jnp.roll(attended, offset, axis=0)
        return (sample.astype(jnp.float32) + attended).astype(jnp.bfloat16)
    residual = lax.map(attend, (tokens, shifts))
    blocks = SAMPLES * N_SPACE
    second_norm = layer_norm(residual.reshape(blocks * TOK_DEV, D), norm2_gain).astype(jnp.bfloat16).reshape(blocks, TOK_DEV, D)
    regime_ids = regimes.reshape(blocks, TOK_DEV).astype(jnp.int32)
    one_hot = (regime_ids[:, :, None] == jnp.arange(EXPERTS, dtype=jnp.int32)[None, None, :]).astype(jnp.int32)
    before = jnp.cumsum(one_hot, axis=1) - one_hot
    slot_index = lax.optimization_barrier(jnp.sum(before * one_hot, axis=2)).astype(jnp.int32)
    target = (regime_ids * CAP + slot_index).astype(jnp.int32)
    row_index = jnp.broadcast_to(jnp.arange(TOK_DEV, dtype=jnp.int32)[None, :], (blocks, TOK_DEV))
    table = jax.vmap(lambda place, row_ids: jnp.zeros((EXPERTS * CAP,), jnp.int32).at[place].set(row_ids))(target, row_index)
    live = jax.vmap(lambda place: jnp.zeros((EXPERTS * CAP,), jnp.int32).at[place].set(1))(target)

    def expert_step(expert_out, expert):
        expert = expert.astype(jnp.int32)
        chosen = lax.dynamic_slice_in_dim(table, expert * CAP, CAP, 1)
        used = lax.dynamic_slice_in_dim(live, expert * CAP, CAP, 1)
        inputs = jax.vmap(lambda source, picks: source[picks])(second_norm, chosen).reshape(blocks * CAP, D)
        pre_act = jnp.dot(inputs, w_in[expert], preferred_element_type=jnp.float32)
        hidden = jax.nn.gelu(pre_act, approximate=False).astype(jnp.bfloat16)
        weight_rows = w_out[expert]
        summed = jnp.zeros((blocks * CAP, D), jnp.float32)
        for group in range(N_MP):
            lower = group * half_hidden
            part_out = jnp.dot(hidden[:, lower:lower + half_hidden], weight_rows[:, lower:lower + half_hidden].T, preferred_element_type=jnp.float32)
            summed = summed + part_out.astype(jnp.bfloat16).astype(jnp.float32)
        values = summed.astype(jnp.bfloat16).reshape(blocks, CAP, D)
        place = jnp.where(used > 0, chosen, TOK_DEV).astype(jnp.int32)
        expert_out = jax.vmap(lambda store, spots, rows_in: store.at[spots].set(rows_in, mode='drop'))(expert_out, place, values)
        return (expert_out, None)
    expert_out, unused = lax.scan(expert_step, jnp.zeros((blocks, TOK_DEV, D), jnp.bfloat16), jnp.arange(EXPERTS, dtype=jnp.int32))
    result = (residual.reshape(blocks, TOK_DEV, D).astype(jnp.float32) + expert_out.astype(jnp.float32)).astype(jnp.bfloat16)
    return result.reshape(SAMPLES, NX, WIN, WIN, D)
```

```python
import jax
import jax.numpy as jnp
from jax import lax
from jax.sharding import PartitionSpec as P

HEAD_DIM = 32


EPS = 1e-05


def from_behind(block, axis, distance):
    devices = range(lax.axis_size(axis))
    route = [((i - distance) % len(devices), i) for i in devices]
    return lax.ppermute(block, axis, route)


def layer_norm(values, gain):
    values = values.astype(jnp.float32)
    center = values - jnp.mean(values, axis=-1, keepdims=True)
    spread = jnp.mean(center * center, axis=-1, keepdims=True)
    return center * lax.rsqrt(spread + EPS) * gain


def one_window(part):
    query = part[:, 0]
    keys = part[:, 1]
    values = part[:, 2]
    scores = jnp.einsum(
        "phc,qhc->hpq", query, keys, preferred_element_type=jnp.float32
    ) * part.shape[-1] ** (-0.5)
    peak = jnp.max(scores, axis=-1, keepdims=True)
    weights = jnp.exp(scores - peak)
    total = jnp.sum(weights, axis=-1, keepdims=True)
    probabilities = (weights / total).astype(jnp.bfloat16)
    context = jnp.einsum("hpq,qhc->phc", probabilities, values, preferred_element_type=jnp.float32)
    return context.astype(jnp.bfloat16).reshape(part.shape[0], part.shape[2] * part.shape[3])


def swap(block):
    return from_behind(block, "mp", 1)


def exchange(blocks, groups):
    me = lax.axis_index("expert")
    arrived = []
    for distance in range(groups):
        part = lax.dynamic_index_in_dim(blocks, (me + distance) % groups, 0, keepdims=False)
        arrived.append(from_behind(part, "expert", distance) if distance else part)
    return arrived


def body(tokens, shifts, regimes, norm1_gain, qkv_weight, out_weight, norm2_gain, w_in, w_out):
    planes = tokens.shape[1]
    window = tokens.shape[2]
    width = tokens.shape[4]
    rim_planes = window - 1
    plane_cells = window * window
    row_count = planes * plane_cells
    core = lax.axis_index("mp")
    with jax.named_scope("gather_in"):
        full_in = lax.all_gather(w_in[0], "space", axis=0, tiled=True)
    with jax.named_scope("gather_out"):
        full_out = lax.all_gather(w_out[0], "space", axis=0, tiled=True)
    own_rows = tokens.reshape(row_count, width)
    half_rim = rim_planes * plane_cells // 2
    rim_mine = from_behind(lax.dynamic_slice_in_dim(own_rows, core * half_rim, half_rim, 0), "space", -1)
    rim_other = swap(rim_mine)
    rim = jnp.where(
        core == 0,
        jnp.concatenate([rim_mine, rim_other], axis=0),
        jnp.concatenate([rim_other, rim_mine], axis=0),
    )
    extended = jnp.concatenate([own_rows, rim], axis=0)
    offset = shifts[0]
    rolled = lax.dynamic_slice_in_dim(extended, offset * plane_cells, row_count, 0)
    normed = layer_norm(rolled, norm1_gain).astype(jnp.bfloat16)
    projected = jnp.einsum(
        "rd,dkc->rkc", normed, qkv_weight, preferred_element_type=jnp.float32
    ).astype(jnp.bfloat16)
    head_width = qkv_weight.shape[2]
    heads_local = head_width // HEAD_DIM
    grouped = projected.reshape(planes // window, window * plane_cells, 3, heads_local, HEAD_DIM)
    context = lax.map(one_window, grouped).reshape(row_count, head_width)
    behind = from_behind(context[row_count - rim_planes * plane_cells :], "space", 1)
    joined = jnp.concatenate([behind, context], axis=0)
    restored = lax.dynamic_slice_in_dim(joined, (rim_planes - offset) * plane_cells, row_count, 0)
    part = jnp.dot(restored, out_weight, preferred_element_type=jnp.float32).astype(jnp.bfloat16)
    attended = part.astype(jnp.float32) + swap(part).astype(jnp.float32)
    residual = (own_rows.astype(jnp.float32) + attended).astype(jnp.bfloat16)
    second_norm = layer_norm(residual, norm2_gain).astype(jnp.bfloat16)

    regime_ids = regimes.reshape(row_count)
    groups = lax.axis_size("expert")
    capacity = 2 * row_count // groups
    half = capacity // 2
    one_hot = (regime_ids[:, None] == jnp.arange(groups, dtype=jnp.int32)[None, :]).astype(jnp.int32)
    before = jnp.cumsum(one_hot, axis=0) - one_hot
    slot_index = jnp.sum(before * one_hot, axis=1)
    side = slot_index // half
    place = regime_ids * half + slot_index % half
    mine = jnp.where(side == core, place, -1)
    spots = jnp.arange(groups * half, dtype=jnp.int32)
    pick = (spots[:, None] == mine[None, :]).astype(jnp.bfloat16)
    buffer = jnp.dot(pick, second_norm, preferred_element_type=jnp.float32).astype(jnp.bfloat16)
    got = jnp.concatenate(exchange(buffer.reshape(groups, half, width), groups), axis=0)
    rows = jnp.concatenate([got, swap(got)], axis=0)
    pre_act = jnp.dot(rows, full_in, preferred_element_type=jnp.float32)
    hidden = jax.nn.gelu(pre_act, approximate=False).astype(jnp.bfloat16)

    cut = width // 2
    theirs = lax.dynamic_slice_in_dim(full_out, (1 - core) * cut, cut, 0)
    ours = lax.dynamic_slice_in_dim(full_out, core * cut, cut, 0)
    dims = (((1,), (1,)), ((), ()))
    sent = lax.dot_general(hidden, theirs, dims, preferred_element_type=jnp.float32).astype(jnp.bfloat16)
    kept = lax.dot_general(hidden, ours, dims, preferred_element_type=jnp.float32).astype(jnp.bfloat16)
    taken = swap(sent)
    mid = groups * half
    taken = jnp.concatenate([taken[mid:], taken[:mid]], axis=0)
    outbound = (kept.astype(jnp.float32) + taken.astype(jnp.float32)).astype(jnp.bfloat16)

    me = lax.axis_index("expert")
    returned = []
    stacked = outbound.reshape(2, groups, half, cut)
    for distance in range(groups):
        block = stacked[:, distance]
        returned.append(from_behind(block, "expert", -distance) if distance else block)
    back = jnp.stack(returned, axis=0).reshape(groups * capacity, cut)
    order = (regime_ids - me) % groups
    swapped = jnp.where(side == core, 0, 1)
    code = order * capacity + swapped * half + slot_index % half
    choose = (code[:, None] == jnp.arange(groups * capacity, dtype=jnp.int32)[None, :]).astype(jnp.bfloat16)
    picked = jnp.dot(choose, back, preferred_element_type=jnp.float32).astype(jnp.bfloat16)
    other = swap(picked)
    expert_out = jnp.where(
        core == 0,
        jnp.concatenate([picked, other], axis=1),
        jnp.concatenate([other, picked], axis=1),
    )
    final = (residual.astype(jnp.float32) + expert_out.astype(jnp.float32)).astype(jnp.bfloat16)
    return final.reshape(tokens.shape)


def solution(mesh):
    return jax.shard_map(
        body,
        mesh=mesh,
        in_specs=(
            P("expert", "space", None, None, None),
            P("expert"),
            P("expert", "space", None, None, None),
            P(),
            P(None, None, "mp"),
            P("mp", None),
            P(),
            P("expert", "space", "mp"),
            P("expert", "space", "mp"),
        ),
        out_specs=P("expert", "space", None, None, None),
        check_vma=False,
    )
```

```python
import jax
import jax.numpy as jnp
from jax import lax
from jax.sharding import PartitionSpec as P

HEAD_DIM = 32


EPS = 1e-05


def from_behind(block, axis, distance):
    devices = range(lax.axis_size(axis))
    route = [((i - distance) % len(devices), i) for i in devices]
    return lax.ppermute(block, axis, route)


def layer_norm(values, gain):
    values = values.astype(jnp.float32)
    center = values - jnp.mean(values, axis=-1, keepdims=True)
    spread = jnp.mean(center * center, axis=-1, keepdims=True)
    return center * lax.rsqrt(spread + EPS) * gain


def one_window(part):
    query = part[:, 0]
    keys = part[:, 1]
    values = part[:, 2]
    scores = jnp.einsum(
        "phc,qhc->hpq", query, keys, preferred_element_type=jnp.float32
    ) * part.shape[-1] ** (-0.5)
    peak = jnp.max(scores, axis=-1, keepdims=True)
    weights = jnp.exp(scores - peak)
    total = jnp.sum(weights, axis=-1, keepdims=True)
    probabilities = (weights / total).astype(jnp.bfloat16)
    context = jnp.einsum("hpq,qhc->phc", probabilities, values, preferred_element_type=jnp.float32)
    return context.astype(jnp.bfloat16).reshape(part.shape[0], part.shape[2] * part.shape[3])


def swap(block):
    return from_behind(block, "mp", 1)


def body(tokens, shifts, regimes, norm1_gain, qkv_weight, out_weight, norm2_gain, w_in, w_out):
    planes = tokens.shape[1]
    window = tokens.shape[2]
    width = tokens.shape[4]
    rim_planes = window - 1
    plane_cells = window * window
    row_count = planes * plane_cells
    core = lax.axis_index("mp")
    with jax.named_scope("gather_in"):
        full_in = lax.all_gather(w_in[0], "space", axis=0, tiled=True)
    parts = 2
    step = w_out.shape[1] // parts
    full_out = []
    for p in range(parts):
        with jax.named_scope(f"gather_out_{p}"):
            full_out.append(lax.all_gather(w_out[0, p * step : (p + 1) * step], "space", axis=0, tiled=True))
    own_rows = tokens.reshape(row_count, width)
    half_rim = rim_planes * plane_cells // 2
    rim_mine = from_behind(lax.dynamic_slice_in_dim(own_rows, core * half_rim, half_rim, 0), "space", -1)
    rim_other = swap(rim_mine)
    rim = jnp.where(
        core == 0,
        jnp.concatenate([rim_mine, rim_other], axis=0),
        jnp.concatenate([rim_other, rim_mine], axis=0),
    )
    extended = jnp.concatenate([own_rows, rim], axis=0)
    offset = shifts[0]
    rolled = lax.dynamic_slice_in_dim(extended, offset * plane_cells, row_count, 0)
    normed = layer_norm(rolled, norm1_gain).astype(jnp.bfloat16)
    projected = jnp.einsum(
        "rd,dkc->rkc", normed, qkv_weight, preferred_element_type=jnp.float32
    ).astype(jnp.bfloat16)
    head_width = qkv_weight.shape[2]
    heads_local = head_width // HEAD_DIM
    grouped = projected.reshape(planes // window, window * plane_cells, 3, heads_local, HEAD_DIM)
    context = lax.map(one_window, grouped).reshape(row_count, head_width)
    behind = from_behind(context[row_count - rim_planes * plane_cells :], "space", 1)
    joined = jnp.concatenate([behind, context], axis=0)
    restored = lax.dynamic_slice_in_dim(joined, (rim_planes - offset) * plane_cells, row_count, 0)
    part = jnp.dot(restored, out_weight, preferred_element_type=jnp.float32).astype(jnp.bfloat16)
    attended = part.astype(jnp.float32) + swap(part).astype(jnp.float32)
    residual = (own_rows.astype(jnp.float32) + attended).astype(jnp.bfloat16)
    second_norm = layer_norm(residual, norm2_gain).astype(jnp.bfloat16)

    regime_ids = regimes.reshape(row_count)
    groups = lax.axis_size("expert")
    capacity = 2 * row_count // groups
    half = capacity // 2
    one_hot = (regime_ids[:, None] == jnp.arange(groups, dtype=jnp.int32)[None, :]).astype(jnp.int32)
    before = jnp.cumsum(one_hot, axis=0) - one_hot
    slot_index = jnp.sum(before * one_hot, axis=1)
    side = slot_index // half
    place = regime_ids * half + slot_index % half
    mine = jnp.where(side == core, place, -1)
    me = lax.axis_index("expert")
    spots = jnp.arange(half, dtype=jnp.int32)

    def rows_for(owner, slots):
        pick = (owner * half + spots)[:, None] == slots[None, :]
        return jnp.dot(
            pick.astype(jnp.bfloat16), second_norm, preferred_element_type=jnp.float32
        ).astype(jnp.bfloat16)

    arrived = [
        from_behind(rows_for((me + distance) % groups, mine), "expert", distance)
        for distance in range(1, groups)
    ]
    theirs_slots = jnp.where(side == core, -1, place)

    def expert_hidden(*chunk):
        pre_act = jnp.dot(
            jnp.concatenate(chunk, axis=0), full_in, preferred_element_type=jnp.float32
        )
        return jax.nn.gelu(pre_act, approximate=False).astype(jnp.bfloat16)

    hidden = [expert_hidden(rows_for(me, mine), rows_for(me, theirs_slots))]
    arrived, hidden[0] = lax.optimization_barrier((arrived, hidden[0]))
    hidden += [expert_hidden(block, swap(block)) for block in arrived]
    hidden = jnp.concatenate(hidden, axis=0)

    order = (regime_ids - me) % groups
    swapped = jnp.where(side == core, 0, 1)
    code = order * capacity + swapped * half + slot_index % half
    choose = (code[:, None] == jnp.arange(groups * capacity, dtype=jnp.int32)[None, :]).astype(jnp.bfloat16)
    dims = (((1,), (1,)), ((), ()))
    low, high = [], []
    for weights in full_out:
        cut = weights.shape[0] // 2
        theirs = lax.dynamic_slice_in_dim(weights, (1 - core) * cut, cut, 0)
        ours = lax.dynamic_slice_in_dim(weights, core * cut, cut, 0)
        sent = lax.dot_general(hidden, theirs, dims, preferred_element_type=jnp.float32).astype(jnp.bfloat16)
        taken = swap(sent).reshape(groups, 2, half, cut)
        kept = lax.dot_general(hidden, ours, dims, preferred_element_type=jnp.float32).astype(jnp.bfloat16)
        kept = kept.reshape(groups, 2, half, cut)
        blocks = []
        for distance in range(groups):
            block = jnp.concatenate(
                [
                    kept[distance, at].astype(jnp.float32) + taken[distance, 1 - at].astype(jnp.float32)
                    for at in range(2)
                ],
                axis=0,
            ).astype(jnp.bfloat16)
            blocks.append(block)
        blocks, hidden = lax.optimization_barrier((blocks, hidden))
        returned = blocks[:1] + [from_behind(blocks[d], "expert", -d) for d in range(1, groups)]
        back = jnp.concatenate(returned, axis=0)
        picked = jnp.dot(choose, back, preferred_element_type=jnp.float32).astype(jnp.bfloat16)
        other = swap(picked)
        low.append(jnp.where(core == 0, picked, other))
        high.append(jnp.where(core == 0, other, picked))
    pieces = []
    for side_parts in (low, high):
        for at in range(0, side_parts[0].shape[1], step):
            pieces += [part[:, at : at + step] for part in side_parts]
    expert_out = jnp.concatenate(pieces, axis=1)
    final = (residual.astype(jnp.float32) + expert_out.astype(jnp.float32)).astype(jnp.bfloat16)
    return final.reshape(tokens.shape)


def solution(mesh):
    return jax.shard_map(
        body,
        mesh=mesh,
        in_specs=(
            P("expert", "space", None, None, None),
            P("expert"),
            P("expert", "space", None, None, None),
            P(),
            P(None, None, "mp"),
            P("mp", None),
            P(),
            P("expert", "space", "mp"),
            P("expert", "space", "mp"),
        ),
        out_specs=P("expert", "space", None, None, None),
        check_vma=False,
    )
```

```python
import jax
import jax.numpy as jnp
from jax import lax
from jax.sharding import PartitionSpec as P


HEAD_DIM = 32


EPS = 1e-05


def from_behind(block, axis, distance):
    devices = range(lax.axis_size(axis))
    route = [((i - distance) % len(devices), i) for i in devices]
    return lax.ppermute(block, axis, route)


def layer_norm(values, gain):
    values = values.astype(jnp.float32)
    center = values - jnp.mean(values, axis=-1, keepdims=True)
    spread = jnp.mean(center * center, axis=-1, keepdims=True)
    return center * lax.rsqrt(spread + EPS) * gain


def one_window(part):
    query = part[:, 0]
    keys = part[:, 1]
    values = part[:, 2]
    scores = jnp.einsum(
        "phc,qhc->hpq", query, keys, preferred_element_type=jnp.float32
    ) * part.shape[-1] ** (-0.5)
    peak = jnp.max(scores, axis=-1, keepdims=True)
    weights = jnp.exp(scores - peak)
    total = jnp.sum(weights, axis=-1, keepdims=True)
    probabilities = (weights / total).astype(jnp.bfloat16)
    context = jnp.einsum("hpq,qhc->phc", probabilities, values, preferred_element_type=jnp.float32)
    return context.astype(jnp.bfloat16).reshape(part.shape[0], part.shape[2] * part.shape[3])


def swap(block):
    return from_behind(block, "mp", 1)


def along(block_up, block_down):
    count = lax.axis_size("space")
    up = lax.ppermute(block_up, "space", [(i + 1, i) for i in range(count - 1)])
    down = lax.ppermute(block_down, "space", [(i, i + 1) for i in range(count - 1)])
    return up, down


def rows_in_order(own, ups, downs):
    count = lax.axis_size("space")
    line = jnp.concatenate(downs[::-1] + [own] + ups, axis=0)
    size = own.shape[0]
    return lax.dynamic_slice_in_dim(line, (count - 1 - lax.axis_index("space")) * size, count * size, 0)


def nearest(own, ups, downs, k):
    me, count = lax.axis_index("space"), lax.axis_size("space")
    below, above = me, count - 1 - me
    short = jnp.minimum(below, above)
    longer_up = above > below
    if k == 0:
        return own, me
    paired = k <= 2 * short
    step = jnp.where(paired, (k + 1) // 2, k - short)
    from_up = jnp.where(paired & (k % 2 == 0), ~longer_up, longer_up)
    shard = None
    for s in range((k + 1) // 2, k + 1):
        option = jnp.where(from_up, ups[s - 1], downs[s - 1])
        shard = option if shard is None else jnp.where(step == s, option, shard)
    return shard, jnp.where(from_up, me + step, me - step)


def layer(tokens, shifts, regimes, norm1_gain, qkv_weight, out_weight, norm2_gain, w_in, w_out):
    planes = tokens.shape[1]
    window = tokens.shape[2]
    width = tokens.shape[4]
    rim_planes = window - 1
    plane_cells = window * window
    row_count = planes * plane_cells
    core = lax.axis_index("mp")
    shards = lax.axis_size("space")
    size = w_out.shape[1] // 2

    def halves(blocks):
        return [
            jnp.concatenate([lax.dynamic_slice_in_dim(w, at * size, size, 0) for w in blocks], axis=0)
            for at in (core, 1 - core)
        ]

    in_up, in_down, out_up, out_down = [], [], [], []

    def advance(own, ups, downs):
        up, down = along(ups[-1] if ups else own, downs[-1] if downs else own)
        ups.append(up)
        downs.append(down)

    own_rows = tokens.reshape(row_count, width)
    half_rim = rim_planes * plane_cells // 2
    rim_mine = from_behind(lax.dynamic_slice_in_dim(own_rows, core * half_rim, half_rim, 0), "space", -1)
    rim_other = swap(rim_mine)
    rim = jnp.where(
        core == 0,
        jnp.concatenate([rim_mine, rim_other], axis=0),
        jnp.concatenate([rim_other, rim_mine], axis=0),
    )
    extended = jnp.concatenate([own_rows, rim], axis=0)
    offset = shifts[0]
    advance(w_in[0], in_up, in_down)
    own_out, extended = lax.optimization_barrier((w_out[0], extended))
    advance(own_out, out_up, out_down)
    rolled = lax.dynamic_slice_in_dim(extended, offset * plane_cells, row_count, 0)
    normed = layer_norm(rolled, norm1_gain).astype(jnp.bfloat16)
    projected = jnp.einsum("rd,dkc->rkc", normed, qkv_weight, preferred_element_type=jnp.float32).astype(jnp.bfloat16)
    head_width = qkv_weight.shape[2]
    heads_local = head_width // HEAD_DIM
    grouped = projected.reshape(planes // window, window * plane_cells, 3, heads_local, HEAD_DIM)
    context = lax.map(one_window, grouped).reshape(row_count, head_width)
    context, in_up, in_down = lax.optimization_barrier((context, in_up, in_down))
    behind = from_behind(context[row_count - rim_planes * plane_cells :], "space", 1)
    advance(w_in[0], in_up, in_down)
    joined = jnp.concatenate([behind, context], axis=0)
    restored = lax.dynamic_slice_in_dim(joined, (rim_planes - offset) * plane_cells, row_count, 0)
    part = jnp.dot(restored, out_weight, preferred_element_type=jnp.float32).astype(jnp.bfloat16)
    attended = part.astype(jnp.float32) + swap(part).astype(jnp.float32)
    residual = (own_rows.astype(jnp.float32) + attended).astype(jnp.bfloat16)
    second_norm = layer_norm(residual, norm2_gain).astype(jnp.bfloat16)

    second_norm, in_up, in_down = lax.optimization_barrier((second_norm, in_up, in_down))
    while len(in_up) < shards - 1:
        advance(w_in[0], in_up, in_down)

    regime_ids = regimes.reshape(row_count)
    groups = lax.axis_size("expert")
    capacity = 2 * row_count // groups
    half = capacity // 2
    one_hot = (regime_ids[:, None] == jnp.arange(groups, dtype=jnp.int32)[None, :]).astype(jnp.int32)
    before = jnp.cumsum(one_hot, axis=0) - one_hot
    slot_index = jnp.sum(before * one_hot, axis=1)
    side = slot_index // half
    place = regime_ids * half + slot_index % half
    mine = jnp.where(side == core, place, -1)
    me = lax.axis_index("expert")
    spots = jnp.arange(half, dtype=jnp.int32)

    def rows_for(owner, slots):
        pick = (owner * half + spots)[:, None] == slots[None, :]
        return jnp.dot(
            pick.astype(jnp.bfloat16), second_norm, preferred_element_type=jnp.float32
        ).astype(jnp.bfloat16)

    arrived = []
    for distance in range(1, groups):
        block = rows_for((me + distance) % groups, mine)
        arrived.append(from_behind(block, "expert", distance))
    theirs_slots = jnp.where(side == core, -1, place)

    full_in = rows_in_order(w_in[0], in_up, in_down)
    full_in, out_up, out_down = lax.optimization_barrier((full_in, out_up, out_down))
    while len(out_up) < shards - 2:
        advance(own_out, out_up, out_down)

    def expert_hidden(*chunk):
        pre_act = jnp.dot(
            jnp.concatenate(chunk, axis=0), full_in, preferred_element_type=jnp.float32
        )
        return jax.nn.gelu(pre_act, approximate=False).astype(jnp.bfloat16)

    own_chunk = rows_for(me, jnp.where(side == core, place, -1)), rows_for(me, theirs_slots)
    hidden = [expert_hidden(*own_chunk)]
    arrived, hidden[0] = lax.optimization_barrier((arrived, hidden[0]))
    hidden += [expert_hidden(block, swap(block)) for block in arrived]
    hidden = jnp.concatenate(hidden, axis=0)
    near = [nearest(own_out, out_up, out_down, k) for k in range(shards - 1)]
    near_weights = halves([w for w, _ in near])
    hidden, out_up, out_down, near_weights = lax.optimization_barrier(
        (hidden, out_up, out_down, near_weights)
    )
    advance(own_out, out_up, out_down)
    last = nearest(own_out, out_up, out_down, shards - 1)

    order = (regime_ids - me) % groups
    swapped = jnp.where(side == core, 0, 1)
    code = order * capacity + swapped * half + slot_index % half
    choose = (code[:, None] == jnp.arange(groups * capacity, dtype=jnp.int32)[None, :]).astype(jnp.bfloat16)
    dims = (((1,), (1,)), ((), ()))
    pieces = {}
    owners = [owner for _, owner in near] + [last[1]]
    for group in (range(shards - 1), range(shards - 1, shards)):
        ours, theirs = near_weights if 0 in group else halves([last[0]])
        cut = ours.shape[0]
        part = "near" if 0 in group else "far"
        sent = lax.dot_general(hidden, theirs, dims, preferred_element_type=jnp.float32).astype(jnp.bfloat16)
        taken = swap(sent).reshape(groups, 2, half, cut)
        kept = lax.dot_general(hidden, ours, dims, preferred_element_type=jnp.float32).astype(jnp.bfloat16)
        kept = kept.reshape(groups, 2, half, cut)
        blocks = []
        for distance in range(groups):
            block = jnp.concatenate(
                [
                    kept[distance, at].astype(jnp.float32) + taken[distance, 1 - at].astype(jnp.float32)
                    for at in range(2)
                ],
                axis=0,
            ).astype(jnp.bfloat16)
            blocks.append(block)
        blocks, hidden = lax.optimization_barrier((blocks, hidden))
        returned = blocks[:1]
        for distance in range(1, groups):
            returned.append(from_behind(blocks[distance], "expert", -distance))
        picked = jnp.dot(choose[:, :capacity], returned[0], preferred_element_type=jnp.float32)
        back = jnp.concatenate(returned[1:], axis=0)
        picked += jnp.dot(choose[:, capacity:], back, preferred_element_type=jnp.float32)
        picked = picked.astype(jnp.bfloat16)
        other = swap(picked)
        left = jnp.where(core == 0, picked, other)
        right = jnp.where(core == 0, other, picked)
        for at, k in enumerate(group):
            cols = slice(at * size, (at + 1) * size)
            pieces[k] = jnp.concatenate([left[:, cols], right[:, cols]], axis=1)
    ordered = []
    for shard in range(shards):
        value = pieces[0]
        for k in range(1, shards):
            value = jnp.where(owners[k] == shard, pieces[k], value)
        ordered.append(value)
    expert_out = jnp.concatenate(ordered, axis=1)
    final = (residual.astype(jnp.float32) + expert_out.astype(jnp.float32)).astype(jnp.bfloat16)
    return final.reshape(tokens.shape)


def solution(mesh):
    return jax.shard_map(
        layer,
        mesh=mesh,
        in_specs=(
            P("expert", "space", None, None, None),
            P("expert"),
            P("expert", "space", None, None, None),
            P(),
            P(None, None, "mp"),
            P("mp", None),
            P(),
            P("expert", "space", "mp"),
            P("expert", "space", "mp"),
        ),
        out_specs=P("expert", "space", None, None, None),
        check_vma=False,
    )
```
